32 devices in a mesh: outer: 4 (over y, x), inner: 8 (over z, core).
Axes of the slice: x: 2, y: 2, z: 4, core: 2. Of those that a mesh axis runs over, the one named last changes fastest.
Arguments:
- queries: bfloat16 [4096, 4096], P(('outer', 'inner')), may hold values from -24 to 24, as said below
- keys: bfloat16 [4096, 1024], P(('outer', 'inner')), may hold values from -24 to 24, as said below
- values: bfloat16 [4096, 1024], P(('outer', 'inner')), may hold values from -6 to 6
Outputs:
- attended: bfloat16 [4096, 4096], P(('outer', 'inner'))
The draws below stay inside these ranges and needn't reach their ends.
Inputs may be any that keep to these rules, and one draw needn't show every extreme that they name: `queries`: entries of order one, a few larger. `keys`: entries of order one, a few larger.
All inputs are finite; a program needn't handle non-finite values.
Results may differ from the reference program's by a relative error of at most 0.008.
Values may be sent and summed in bfloat16 or wider, within the bound.
No kernel may reach another device: no remote copies, remote signals or barrier semaphores. Data moves between devices by JAX's collectives and lax.ppermute only.
A program may use at most 128 MiB of HBM per device.

```python
import jax
import jax.numpy as jnp
from jax import lax

QH = 32
KVH = 8
HD = 128
TOK_DEV = 128
TOKENS = 4096
N_OUTER = 4
N_INNER = 8


def shared_fields(key):
    base = jax.random.fold_in(key, 11)
    ratio = QH // KVH
    key_noise = jnp.clip(jax.random.normal(jax.random.fold_in(base, 1), (TOKENS, KVH, HD), jnp.float32), -6.0, 6.0)
    query_noise = jnp.clip(jax.random.normal(jax.random.fold_in(base, 2), (TOKENS, KVH, ratio, HD), jnp.float32), -6.0, 6.0)
    key_noise = jnp.clip(key_noise, -24.0, 24.0)
    query_noise = jnp.clip(query_noise, -24.0, 24.0)
    return (query_noise, key_noise)


def draw_queries(key, part):
    query_noise, key_noise = shared_fields(key)
    return query_noise.reshape(TOKENS, QH * HD).astype(jnp.bfloat16)


def draw_keys(key, part):
    query_noise, key_noise = shared_fields(key)
    return key_noise.reshape(TOKENS, KVH * HD).astype(jnp.bfloat16)


def shard_levels(rng, shape, shards, smallest, top_value):
    def one(dim, shards_of):
        heights = jax.random.uniform(jax.random.fold_in(jax.random.fold_in(rng, 6), dim), (shards_of,), jnp.float32, smallest / len(shards), top_value / len(shards))
        return jnp.repeat(jnp.exp(heights), shape[dim] // shards_of).reshape((-1,) + (1,) * (len(shape) - dim - 1))

    factor_of = one(*shards[0])
    for cut in shards[1:]:
        factor_of = factor_of * one(*cut)
    return factor_of


def gaussian(stream_key, dims, scale, bound, split=(), held_as=jnp.bfloat16):
    values = scale * jax.random.normal(stream_key, dims, jnp.float32)
    if split:
        values = values * shard_levels(stream_key, dims, split, -0.22, 0.18)
    return jnp.clip(values, -bound, bound).astype(held_as)


def setup_inputs(seed: int = 0) -> dict:
    key_of = jax.random.split(jax.random.key(seed), 4)
    queries = draw_queries(jax.random.fold_in(key_of[3], 71), 0)
    keys = draw_keys(jax.random.fold_in(key_of[3], 71), 0)
    values = gaussian(key_of[2], (TOKENS, KVH * HD), 1.0, 6.0, ((0, 32),))
    return dict(queries=queries, keys=keys, values=values)


def reference(queries, keys, values):
    group = TOK_DEV * N_INNER
    length = group * N_OUTER
    ratio = QH // KVH
    scale = 1.0 / (HD ** 0.5)
    padded_keys = jnp.pad(keys.reshape(length, KVH, HD), ((group, group), (0, 0), (0, 0)))
    padded_values = jnp.pad(values.reshape(length, KVH, HD), ((group, group), (0, 0), (0, 0)))
    block = 256 if group % 256 == 0 else group
    blocks = length // block

    def one_block(index):
        start = (index * block).astype(jnp.int32)
        owner = (start // group).astype(jnp.int32)
        rows = lax.dynamic_slice_in_dim(queries, start, block, 0)
        rows = rows.reshape(block, KVH, ratio, HD).astype(jnp.float32)
        near_keys = lax.dynamic_slice_in_dim(padded_keys, (owner * group).astype(jnp.int32), 3 * group, 0).astype(jnp.float32)
        near_values = lax.dynamic_slice_in_dim(padded_values, (owner * group).astype(jnp.int32), 3 * group, 0).astype(jnp.float32)
        scores = jnp.einsum("qgrd,kgd->grqk", rows, near_keys) * scale
        source = owner - 1 + (jnp.arange(3 * group, dtype=jnp.int32) // group)
        inside = (source >= 0) & (source < N_OUTER)
        scores = jnp.where(inside, scores, -jnp.inf)
        peak = jnp.max(scores, axis=-1, keepdims=True)
        weights = jnp.exp(scores - peak)
        total = jnp.sum(weights, axis=-1)
        rounded = weights.astype(jnp.bfloat16).astype(jnp.float32)
        mixed = jnp.einsum("grqk,kgd->grqd", rounded, near_values) / total[..., None]
        return mixed.transpose(2, 0, 1, 3).reshape(block, QH * HD).astype(jnp.bfloat16)

    result = lax.map(one_block, jnp.arange(blocks, dtype=jnp.int32))
    return result.reshape(length, QH * HD)
```

```python
import functools

import jax
import jax.numpy as jnp
from jax import lax
from jax.experimental import pallas as pl
from jax.experimental.pallas import tpu as pltpu
from jax.sharding import PartitionSpec as P

QH = 32
KVH = 8
HD = 128
SPLIT = 4
LOG2E = 1.4426950408889634


def swap(block, axis, bits):
    count = lax.axis_size(axis)
    return lax.ppermute(block, axis, [(i, i ^ bits) for i in range(count)])


def relay(block, axis):
    count = lax.axis_size(axis)
    route = []
    for i in range(count):
        target = i + 2 if i % 2 == 0 else i - 2
        if 0 <= target < count:
            route.append((i, target))
    return lax.ppermute(block, axis, route)


def columns(array, start, width):
    return lax.dynamic_slice_in_dim(array, start, width, 1)


def attend_kernel(first, last, pieces, sources, *refs):
    flag = refs[0]
    q_refs = refs[1 : 1 + sources]
    kv_refs = refs[1 + sources : 1 + sources + pieces]
    at = 1 + sources + pieces
    if not first:
        peak_in, total_in, accum_in = refs[at : at + 3]
        at += 3
    if last:
        out_refs = refs[at : at + sources]
        at += sources
    else:
        peak_out, total_out, accum_out = refs[at : at + 3]
        at += 3
    ratio = QH // KVH
    rows = q_refs[0].shape[0]
    factor = LOG2E / HD**0.5

    def finish(s, accum, total):
        mixed = (accum / total).astype(jnp.bfloat16)
        for r in range(ratio):
            out_refs[s][:, r * HD : (r + 1) * HD] = mixed[r * rows : (r + 1) * rows]

    def compute():
        values = [
            jnp.concatenate([ref[1], jnp.ones_like(ref[1])], axis=1) for ref in kv_refs
        ]
        for s in range(sources):
            q = jnp.concatenate(
                [q_refs[s][:, r * HD : (r + 1) * HD] for r in range(ratio)], axis=0
            )
            scores = [
                lax.dot_general(
                    q, ref[0], (((1,), (1,)), ((), ())), preferred_element_type=jnp.float32
                )
                for ref in kv_refs
            ]
            peak = functools.reduce(
                jnp.maximum, [jnp.max(x, axis=1, keepdims=True) for x in scores]
            )
            if not first:
                old = peak_in[0, s][:, :1]
                peak = jnp.maximum(peak, old)
            update = 0.0
            for x, v in zip(scores, values):
                weights = jnp.exp2((x - peak) * factor).astype(jnp.bfloat16)
                update = update + jnp.dot(weights, v, preferred_element_type=jnp.float32)
            accum, total = update[:, :HD], update[:, HD:]
            if not first:
                shrink = jnp.exp2((old - peak) * factor)
                accum = accum + accum_in[0, s] * shrink
                total = total + total_in[0, s] * shrink
            if last:
                finish(s, accum, total)
            else:
                peak_out[0, s] = jnp.broadcast_to(peak, total.shape)
                total_out[0, s] = total
                accum_out[0, s] = accum

    if first:
        compute()
        return

    pl.when(flag[0] != 0)(compute)

    @pl.when(flag[0] == 0)
    def _():
        for s in range(sources):
            if last:
                finish(s, accum_in[0, s], total_in[0, s])
            else:
                peak_out[0, s] = peak_in[0, s]
                total_out[0, s] = total_in[0, s]
                accum_out[0, s] = accum_in[0, s]


def attend(flag, qs, kvs, state, last):
    ratio = QH // KVH
    sources, pieces = len(qs), len(kvs)
    heads = kvs[0].shape[2] // HD
    rows, width = qs[0].shape
    keys = kvs[0].shape[1]
    first = state is None
    q_spec = pl.BlockSpec((rows, ratio * HD), lambda j, f: (0, j))
    kv_spec = pl.BlockSpec((2, keys, HD), lambda j, f: (0, 0, j))
    state_spec = pl.BlockSpec((1, sources, ratio * rows, HD), lambda j, f: (j, 0, 0, 0))
    state_shape = jax.ShapeDtypeStruct((heads, sources, ratio * rows, HD), jnp.float32)
    in_specs = [q_spec] * sources + [kv_spec] * pieces + ([] if first else [state_spec] * 3)
    if last:
        out_specs = [q_spec] * sources
        out_shape = [jax.ShapeDtypeStruct((rows, width), jnp.bfloat16)] * sources
    else:
        out_specs = [state_spec] * 3
        out_shape = [state_shape] * 3
    total_rows = heads * ratio * rows * sources
    total_keys = pieces * keys
    return pl.pallas_call(
        functools.partial(attend_kernel, first, last, pieces, sources),
        grid_spec=pltpu.PrefetchScalarGridSpec(
            num_scalar_prefetch=1, grid=(heads,), in_specs=in_specs, out_specs=out_specs
        ),
        out_shape=out_shape,
        cost_estimate=pl.CostEstimate(
            flops=4 * total_rows * total_keys * HD,
            transcendentals=total_rows * total_keys,
            bytes_accessed=4 * total_rows * HD * 4,
        ),
        compiler_params=pltpu.CompilerParams(vmem_limit_bytes=40 * 2**20),
        name="attend_last" if last else "attend_first" if first else "attend_next",
    )(flag, *qs, *kvs, *(() if first else state))


def shards(queries, keys, values):
    position = lax.axis_index("outer")
    groups = lax.axis_size("outer")
    members = lax.axis_size("inner")
    me = lax.axis_index("inner")
    core, side = me % 2, me // 2 % 2
    q_width = queries.shape[1] // SPLIT
    kv_width = keys.shape[1] // SPLIT

    def core_part(which):
        parts = [columns(x, which * 2 * kv_width, 2 * kv_width) for x in (keys, values)]
        return jnp.stack(parts)

    kept = core_part(core)
    came = swap(core_part(1 - core), "inner", 1)
    chip = jnp.concatenate([kept, came], axis=1)
    same = lax.dynamic_slice_in_dim(chip, side * kv_width, kv_width, 2)
    other = lax.dynamic_slice_in_dim(chip, (1 - side) * kv_width, kv_width, 2)

    def quarter(which):
        return columns(queries, ((which % 2) * 2 + which // 2 % 2) * q_width, q_width)

    near = [same] + [
        swap(other if hop % 2 else same, "inner", 2 * hop) for hop in range(1, members // 2)
    ]
    qs = [quarter(me)] + [swap(quarter(me ^ bits), "inner", bits) for bits in range(1, SPLIT)]

    side_group = [swap(piece, "outer", 1) for piece in near]
    far_group = [relay(piece, "outer") for piece in side_group]
    far_ok = jnp.where(position % 2 == 0, position > 0, position < groups - 1)
    far_flag = far_ok.astype(jnp.int32).reshape(1)
    always = jnp.ones((1,), jnp.int32)

    state = attend(always, qs, near, None, False)
    state = attend(always, qs, side_group, state, False)
    outs = attend(far_flag, qs, far_group, state, True)
    outs = [outs[0]] + [swap(outs[bits], "inner", bits) for bits in range(1, SPLIT)]

    result = jnp.zeros_like(queries)
    for bits in range(SPLIT):
        which = me ^ bits
        start = ((which % 2) * 2 + which // 2 % 2) * q_width
        result = lax.dynamic_update_slice_in_dim(result, outs[bits], start, 1)
    return result


def solution(mesh):
    placed = P(("outer", "inner"), None)
    return jax.shard_map(
        shards, mesh=mesh, in_specs=(placed, placed, placed), out_specs=placed, check_vma=False
    )
```
